512 devices in a mesh: af: 32 (over z_hi, x, core), ta: 16 (over y, z_lo).
Axes of the slice: x: 4, y: 8, z: 8 (z_hi: 4, z_lo: 2; z = z_hi * 2 + z_lo), core: 2. Of those that a mesh axis runs over, the one named last changes fastest.
Arguments:
- samples: bfloat16 [4096, 512, 512], P('ta', 'af'), may hold values from -6 to 6
Outputs:
- visibility: float32 [512, 128, 512], P('ta', 'af')
The draws below stay inside these ranges and needn't reach their ends.
All inputs are finite; a program needn't handle non-finite values.
Results may differ from the reference program's by a relative error of at most 0.0022.
Values may be sent and summed in bfloat16 or wider, within the bound.
A program may use at most 64 MiB of HBM per device.

```python
import math
import jax
import jax.numpy as jnp

NI = 512
SAMP = 512
CH = 128
TAPS = 4
F_DEV = 256
FRAMES = 4096
N_TA = 16


def block_levels(key, shape, cuts, least, high):
    level, own = 1.0, jax.random.fold_in(key, 6)
    for axis_at, shards_of in cuts:
        draws = jnp.exp(jax.random.uniform(jax.random.fold_in(own, axis_at), (shards_of,), jnp.float32, least / len(cuts), high / len(cuts)))
        level = level * jnp.repeat(draws, shape[axis_at] // shards_of).reshape([-1 if axis == axis_at else 1 for axis in range(len(shape))])
    return level


def scatter_about(key, dims, scale, bound, pieces=(), held_as=jnp.bfloat16):
    values = jax.random.normal(key, dims, jnp.float32) * scale
    if len(pieces) > 0:
        values = block_levels(key, dims, pieces, -0.22, 0.18) * values
    return jnp.clip(values, min=-bound, max=bound).astype(held_as)


def setup_inputs(seed: int = 0) -> dict:
    streams_of = jax.random.split(jax.random.key(seed), 2)
    samples = scatter_about(streams_of[0], (FRAMES, NI, SAMP), 1.0, 6.0, ((0, 16), (1, 32)))
    return dict(samples=samples)


def tap_window(taps, samp_len):
    points = jnp.arange(taps * samp_len).astype(jnp.float32)
    centre = (taps * samp_len - 1) / 2.0
    shape_part = jnp.sinc((points - centre) / samp_len)
    taper = jnp.square(jnp.sin(math.pi * (points + 0.5) / (taps * samp_len)))
    return (shape_part * taper).reshape(taps, samp_len)

def dft_table(samp_len, channels):
    sample_idx = jnp.arange(samp_len).astype(jnp.int32)[:, None]
    chan_idx = jnp.arange(channels).astype(jnp.int32)[None, :]
    phase = (sample_idx * chan_idx % samp_len).astype(jnp.float32) * (2.0 * math.pi / samp_len)
    scale = 1.0 / math.sqrt(samp_len)
    both = jnp.stack([jnp.cos(phase) * scale, -jnp.sin(phase) * scale], axis=2)
    return both.reshape(samp_len, 2 * channels).astype(jnp.bfloat16)

def reference(samples):
    weights = tap_window(TAPS, SAMP)
    table = dft_table(SAMP, CH)
    padded = jnp.concatenate([jnp.zeros((TAPS - 1, NI, SAMP), jnp.bfloat16), samples], axis=0)
    real_sum = jnp.zeros((CH, NI, NI), jnp.float32)
    imag_sum = jnp.zeros((CH, NI, NI), jnp.float32)
    for block in range(N_TA):
        piece = padded[block * F_DEV:block * F_DEV + F_DEV + TAPS - 1]
        filtered = jnp.zeros((F_DEV, NI, SAMP), jnp.float32)
        for tap in range(TAPS):
            filtered = filtered + weights[tap][None, None, :] * piece[tap:tap + F_DEV].astype(jnp.float32)
        filtered = filtered.astype(jnp.bfloat16)
        spectrum = jnp.dot(filtered.reshape(F_DEV * NI, SAMP), table, preferred_element_type=jnp.float32)
        spectrum = spectrum.astype(jnp.bfloat16).reshape(F_DEV, NI, CH, 2).astype(jnp.float32)
        real_part = spectrum[:, :, :, 0]
        imag_part = spectrum[:, :, :, 1]
        real_sum = real_sum + jnp.einsum('fic,fjc->cij', real_part, real_part) + jnp.einsum('fic,fjc->cij', imag_part, imag_part)
        imag_sum = imag_sum + jnp.einsum('fic,fjc->cij', imag_part, real_part) - jnp.einsum('fic,fjc->cij', real_part, imag_part)
    row_idx = jnp.arange(NI)[:, None]
    col_idx = jnp.arange(NI)[None, :]
    packed = jnp.where((row_idx <= col_idx)[None], real_sum, imag_sum) / FRAMES
    return jnp.transpose(packed, (1, 0, 2))
```

```python
import functools
import math

import jax
import jax.numpy as jnp
import numpy as np
from jax import lax
from jax.experimental import pallas as pl
from jax.experimental.pallas import tpu as pltpu
from jax.sharding import PartitionSpec as P

CH = 128
TAPS = 4
MESH = pl.DeviceIdType.MESH
NX, NZ, NY, NCORE = 4, 8, 8, 2
PEERS = NX * NZ * NCORE
STAGES = 2


def tap_window(taps, samp_len):
    points = np.arange(taps * samp_len).astype(np.float64)
    centre = (taps * samp_len - 1) / 2.0
    shape_part = np.sinc((points - centre) / samp_len)
    taper = np.square(np.sin(math.pi * (points + 0.5) / (taps * samp_len)))
    return (shape_part * taper).reshape(taps, samp_len).astype(np.float32)


def dft_table(samp_len, channels):
    sample_idx = np.arange(samp_len)[:, None]
    chan_idx = np.arange(channels)[None, :]
    phase = (sample_idx * chan_idx % samp_len) * (2.0 * math.pi / samp_len)
    scale = 1.0 / math.sqrt(samp_len)
    both = np.stack([np.cos(phase) * scale, -np.sin(phase) * scale], axis=2)
    both = both.reshape(samp_len, channels // STAGES, STAGES, 2)
    both = both.transpose(0, 2, 1, 3)
    return both.reshape(samp_len, 2 * channels).astype(jnp.bfloat16)


def place():
    af, ta = lax.axis_index("af"), lax.axis_index("ta")
    return af // 8 * 2 + ta % 2, af // 2 % NX, af % 2, ta // 2


def turn_peer(step):
    z, x, core, y = place()
    turn = step % NZ
    ahead = jnp.where(turn % 2 == 1, (turn + 1) // 2, NZ - turn // 2)
    z = (z + ahead) % NZ
    rest = step // NZ
    x = (x + rest // NCORE) % NX
    core = (core + rest % NCORE) % NCORE
    return z // 2 * 8 + x * 2 + core, y * 2 + z % 2, z % 2


def correlate_kernel(
    spec_ref, out_ref, held, part, gathered, total, finals,
    turn_send, turn_recv, row_send, row_recv, swap_send, swap_recv,
):
    z, x, core, y = place()
    af, ta = lax.axis_index("af"), lax.axis_index("ta")
    z_lo = z % 2
    inputs, frames = spec_ref.shape[3], spec_ref.shape[4]
    all_inputs = held.shape[2]
    rows = all_inputs // NY
    half = rows // 2

    barrier = pltpu.get_barrier_semaphore()

    @pl.loop(1, PEERS)
    def _(step):
        to_af, to_ta, _ = turn_peer(step)
        pl.semaphore_signal(
            barrier, inc=1, device_id={"af": to_af, "ta": to_ta}, device_id_type=MESH
        )

    @pl.loop(1, NY)
    def _(step):
        to_ta = (y + step) % NY * 2 + z_lo
        pl.semaphore_signal(
            barrier, inc=1, device_id={"af": af, "ta": to_ta}, device_id_type=MESH
        )

    pl.semaphore_wait(barrier, PEERS - 1 + NY - 1)

    my_rows = pl.ds(pl.multiple_of(af * inputs, inputs), inputs)
    my_frames = pl.ds(pl.multiple_of(z_lo * frames, frames), frames)
    for stage in range(STAGES):
        pltpu.make_async_copy(
            spec_ref.at[stage, af * 2 + z_lo],
            held.at[stage, :, my_rows, my_frames],
            turn_recv.at[stage],
        ).start()

        @pl.loop(1, PEERS)
        def _(step):
            to_af, to_ta, to_lo = turn_peer(step)
            pltpu.make_async_remote_copy(
                src_ref=spec_ref.at[stage, to_af * 2 + to_lo],
                dst_ref=held.at[stage, :, my_rows, my_frames],
                send_sem=turn_send.at[stage],
                recv_sem=turn_recv.at[stage],
                device_id={"af": to_af, "ta": to_ta},
                device_id_type=MESH,
            ).start()

    nt = (((1,), (1,)), ((), ()))

    def dot(a, b):
        return lax.dot_general(a, b, nt, preferred_element_type=jnp.float32)

    side = all_inputs // 2
    row_idx = lax.broadcasted_iota(jnp.int32, (side, side), 0)
    col_idx = lax.broadcasted_iota(jnp.int32, (side, side), 1)
    upper = row_idx <= col_idx
    lo, hi = pl.ds(0, side), pl.ds(side, side)

    def send_rows(stage, first, last):
        @pl.loop(first, last)
        def _(to_y):
            block = pl.ds(pl.multiple_of(to_y * rows, rows), rows)

            @pl.when(to_y != y)
            def _():
                pltpu.make_async_remote_copy(
                    src_ref=part.at[stage, block],
                    dst_ref=gathered.at[stage, y],
                    send_sem=row_send.at[stage],
                    recv_sem=row_recv.at[stage],
                    device_id={"af": af, "ta": to_y * 2 + z_lo},
                    device_id_type=MESH,
                ).start()

            @pl.when(to_y == y)
            def _():
                pltpu.make_async_copy(
                    part.at[stage, block], gathered.at[stage, y], row_recv.at[stage]
                ).start()

    for stage in range(STAGES):
        pltpu.make_async_copy(held.at[stage], held.at[stage], turn_recv.at[stage]).wait()
        for own, other in ((lo, hi), (hi, lo)):
            a, b = held[stage, 0, own], held[stage, 1, own]
            c, d = held[stage, 0, other], held[stage, 1, other]
            real = dot(a, a) + dot(b, b)
            imag = dot(b, a) - dot(a, b)
            part[stage, own, own] = jnp.where(upper, real, imag).astype(part.dtype)
            if own is lo:
                part[stage, own, other] = (dot(a, c) + dot(b, d)).astype(part.dtype)
                send_rows(stage, 0, NY // 2)
            else:
                part[stage, own, other] = (dot(b, c) - dot(a, d)).astype(part.dtype)
                send_rows(stage, NY // 2, NY)

    scale = 1.0 / (frames * lax.axis_size("ta"))
    own_half = pl.ds(pl.multiple_of(z_lo * half, half), half)
    other_half = pl.ds(pl.multiple_of((1 - z_lo) * half, half), half)
    for stage in range(STAGES):
        pltpu.make_async_copy(
            gathered.at[stage], gathered.at[stage], row_recv.at[stage]
        ).wait()
        acc = gathered[stage, 0].astype(jnp.float32)
        for k in range(1, NY):
            acc = acc + gathered[stage, k].astype(jnp.float32)
        total[stage] = acc * scale
        pltpu.make_async_remote_copy(
            src_ref=total.at[stage, other_half],
            dst_ref=finals.at[z_lo * STAGES + stage],
            send_sem=swap_send.at[stage],
            recv_sem=swap_recv.at[stage],
            device_id={"af": af, "ta": y * 2 + 1 - z_lo},
            device_id_type=MESH,
        ).start()
        pltpu.make_async_copy(
            total.at[stage, own_half],
            finals.at[z_lo * STAGES + stage],
            swap_recv.at[stage],
        ).start()

    for stage in range(STAGES):
        both = finals.at[pl.ds(0, 2)]
        pltpu.make_async_copy(both, both, swap_recv.at[stage]).wait()
    for k in range(2 * STAGES):
        out_ref[:, k, :] = finals[k]

    for stage in range(STAGES):
        sent = spec_ref.at[stage, pl.ds(0, PEERS - 1)]
        pltpu.make_async_copy(sent, sent, turn_send.at[stage]).wait()
        sent = gathered.at[stage, pl.ds(0, NY - 1)]
        pltpu.make_async_copy(sent, sent, row_send.at[stage]).wait()
        sent = finals.at[0]
        pltpu.make_async_copy(sent, sent, swap_send.at[stage]).wait()


def correlate(spectrum):
    _, _, _, inputs, frames = spectrum.shape
    all_inputs = inputs * lax.axis_size("af")
    rows = all_inputs // NY
    dma = pltpu.SemaphoreType.DMA
    return pl.pallas_call(
        correlate_kernel,
        out_shape=jax.ShapeDtypeStruct((rows // 2, 2 * STAGES, all_inputs), jnp.float32),
        in_specs=[pl.BlockSpec(memory_space=pltpu.VMEM)],
        out_specs=pl.BlockSpec(memory_space=pltpu.VMEM),
        scratch_shapes=[
            pltpu.VMEM((STAGES, 2, all_inputs, 2 * frames), jnp.bfloat16),
            pltpu.VMEM((STAGES, all_inputs, all_inputs), jnp.bfloat16),
            pltpu.VMEM((STAGES, NY, rows, all_inputs), jnp.bfloat16),
            pltpu.VMEM((STAGES, rows, all_inputs), jnp.float32),
            pltpu.VMEM((2 * STAGES, rows // 2, all_inputs), jnp.float32),
            dma((STAGES,)), dma((STAGES,)), dma((STAGES,)),
            dma((STAGES,)), dma((STAGES,)), dma((STAGES,)),
        ],
        compiler_params=pltpu.CompilerParams(
            collective_id=0, has_side_effects=True, vmem_limit_bytes=48 * 2**20
        ),
    )(spectrum)


def passed_along(value, axis, steps):
    count = lax.axis_size(axis)
    first, last = (max(0, -steps), min(count, count - steps))
    return lax.ppermute(value, axis, [(source, source + steps) for source in range(first, last)])


def filtered_by(weights, extended, frames):
    total = jnp.zeros((frames,) + extended.shape[1:], jnp.float32)
    for tap in range(TAPS):
        total = total + weights[tap][None, None, :] * extended[tap : tap + frames].astype(
            jnp.float32
        )
    return total.astype(jnp.bfloat16)


def on_device(samples):
    frames, inputs, samp_len = samples.shape
    weights = jnp.asarray(tap_window(TAPS, samp_len))
    halo = TAPS - 1
    earlier = passed_along(samples[frames - halo :], "ta", 1)
    padded = jnp.pad(samples, ((halo, 0), (0, 0), (0, 0)))
    filtered = filtered_by(weights, padded, frames)
    first = filtered_by(weights, jnp.concatenate([earlier, samples[:halo]], axis=0), halo)
    filtered = lax.dynamic_update_slice(filtered, first, (0, 0, 0))
    table = jnp.asarray(dft_table(samp_len, CH))
    spectrum = jnp.einsum("nc,fin->cif", table, filtered, preferred_element_type=jnp.float32)
    spectrum = spectrum.astype(jnp.bfloat16)
    spectrum = spectrum.reshape(STAGES, PEERS, 2, inputs, frames)
    return correlate(spectrum)


def solution(mesh):
    in_specs = (P("ta", "af", None),)
    out_specs = P("ta", "af", None)
    return jax.shard_map(
        on_device, mesh=mesh, in_specs=in_specs, out_specs=out_specs, check_vma=False
    )
```

```python
import functools
import math

import jax
import jax.numpy as jnp
import numpy as np
from jax import lax
from jax.experimental import pallas as pl
from jax.experimental.pallas import tpu as pltpu
from jax.sharding import PartitionSpec as P

CH = 128
TAPS = 4
MESH = pl.DeviceIdType.MESH
NX, NZ, NY, NCORE = 4, 8, 8, 2
PEERS = NX * NZ * NCORE
STAGES = 2
CHUNKS = 2
BLOCK = 16


def tap_window(taps, samp_len):
    points = np.arange(taps * samp_len).astype(np.float64)
    centre = (taps * samp_len - 1) / 2.0
    shape_part = np.sinc((points - centre) / samp_len)
    taper = np.square(np.sin(math.pi * (points + 0.5) / (taps * samp_len)))
    return (shape_part * taper).reshape(taps, samp_len).astype(np.float32)


def dft_table(samp_len, channels):
    sample_idx = np.arange(samp_len)[:, None]
    chan_idx = np.arange(channels)[None, :]
    phase = (sample_idx * chan_idx % samp_len) * (2.0 * math.pi / samp_len)
    scale = 1.0 / math.sqrt(samp_len)
    both = np.stack([np.cos(phase) * scale, -np.sin(phase) * scale], axis=2)
    both = both.reshape(samp_len, channels // STAGES, STAGES, 2)
    both = both.transpose(0, 2, 1, 3)
    return both.reshape(samp_len, 2 * channels).astype(jnp.bfloat16)


def place():
    af, ta = lax.axis_index("af"), lax.axis_index("ta")
    z = lax.div(af, 8) * 2 + lax.rem(ta, 2)
    return z, lax.rem(lax.div(af, 2), NX), lax.rem(af, 2), lax.div(ta, 2)


def turn_peer(step):
    z, x, core, y = place()
    turn, rest = lax.rem(step, NZ), lax.div(step, NZ)
    odd = lax.rem(turn, 2)
    hop = lax.div(turn + 1, 2)
    z = lax.rem(z + odd * hop + (1 - odd) * (NZ - hop), NZ)
    x = lax.rem(x + lax.div(rest, NCORE), NX)
    core = lax.rem(core + rest, NCORE)
    z_lo = lax.rem(z, 2)
    return lax.div(z, 2) * 8 + x * 2 + core, y * 2 + z_lo, z_lo


def correlate_kernel(
    x_hbm, w_hbm, t_hbm, out_ref,
    window, table, samples, halo, filtered, spectra, turned, spec,
    held, part, gathered, total, finals,
    load_sem, halo_send, halo_recv,
    turn_send, turn_recv, row_send, row_recv, swap_send, swap_recv,
):
    z, x, core, y = place()
    af, ta = lax.axis_index("af"), lax.axis_index("ta")
    z_lo = lax.rem(z, 2)
    n_ta = lax.axis_size("ta")
    frames, inputs, samp_len = x_hbm.shape
    edge = TAPS - 1
    chunk = frames // CHUNKS
    all_inputs = held.shape[2]
    rows = all_inputs // NY
    half = rows // 2

    loads = [
        pltpu.make_async_copy(w_hbm, window, load_sem.at[0]),
        pltpu.make_async_copy(t_hbm, table, load_sem.at[1]),
        pltpu.make_async_copy(
            x_hbm.at[pl.ds(chunk - edge, chunk + edge)],
            samples.at[pl.ds(chunk, chunk + edge)],
            load_sem.at[2],
        ),
        pltpu.make_async_copy(
            x_hbm.at[pl.ds(0, chunk - edge)],
            samples.at[pl.ds(edge, chunk - edge)],
            load_sem.at[3],
        ),
    ]
    for load in loads:
        load.start()

    barrier = pltpu.get_barrier_semaphore()

    def greet(to_af, to_ta):
        pl.semaphore_signal(
            barrier, inc=1, device_id={"af": to_af, "ta": to_ta}, device_id_type=MESH
        )

    @pl.loop(1, PEERS)
    def _(step):
        to_af, to_ta, _ = turn_peer(step)
        greet(to_af, to_ta)

    @pl.loop(1, NY)
    def _(step):
        greet(af, lax.rem(y + step, NY) * 2 + z_lo)

    after, before = lax.rem(ta + 1, n_ta), lax.rem(ta + n_ta - 1, n_ta)
    greet(af, after)
    greet(af, before)
    n_greet = PEERS - 1 + NY - 1 + 2

    my_rows = pl.ds(pl.multiple_of(af * inputs, inputs), inputs)

    def send_spectra(k, stage):
        start = pl.multiple_of(z_lo * frames + k * chunk, chunk)
        target = held.at[stage, :, my_rows, pl.ds(start, chunk)]
        pltpu.make_async_copy(
            spec.at[k, stage, af * 2 + z_lo], target, turn_recv.at[stage]
        ).start()

        @pl.loop(1, PEERS)
        def _(step):
            to_af, to_ta, to_lo = turn_peer(step)
            pltpu.make_async_remote_copy(
                src_ref=spec.at[k, stage, to_af * 2 + to_lo],
                dst_ref=target,
                send_sem=turn_send.at[stage],
                recv_sem=turn_recv.at[stage],
                device_id={"af": to_af, "ta": to_ta},
                device_id_type=MESH,
            ).start()

    def channelize(first, count):
        base = lax.div(first, chunk) * chunk

        @pl.loop(0, count)
        def _(step):
            f0 = first + (count - 1 - step) * BLOCK
            for lane in range(samp_len // 128):
                cols = pl.ds(lane * 128, 128)
                taps = [
                    jnp.broadcast_to(window[pl.ds(p, 1), cols], (inputs, 128))
                    for p in range(TAPS)
                ]
                recent = [samples[f0 + p, :, cols].astype(jnp.float32) for p in range(edge)]
                for f in range(BLOCK):
                    recent.append(samples[f0 + f + edge, :, cols].astype(jnp.float32))
                    acc = taps[0] * recent[0]
                    for p in range(1, TAPS):
                        acc = acc + taps[p] * recent[p]
                    filtered[pl.ds(f * inputs, inputs), cols] = acc.astype(jnp.bfloat16)
                    recent = recent[1:]
            block = jnp.dot(filtered[...], table[...], preferred_element_type=jnp.float32)
            at = pl.ds(pl.multiple_of((f0 - base) * inputs, BLOCK * inputs), BLOCK * inputs)
            for stage in range(STAGES):
                spectra[stage, at, :] = block[:, stage * 128 : (stage + 1) * 128]

    def arrange(k, stage):
        for i in range(inputs):
            by_frame = spectra[stage, pl.ds(i, chunk, stride=inputs), :]
            turned[pl.ds(i, 128, stride=inputs), :] = by_frame.T
        pieces = turned[...].astype(jnp.bfloat16)
        spec[k, stage] = pieces.reshape(spec.shape[2:])

    for load in loads[:3]:
        load.wait()
    per_chunk = chunk // BLOCK
    channelize(chunk, per_chunk)
    arrange(1, 0)

    pl.semaphore_wait(barrier, n_greet)
    ahead = pltpu.make_async_remote_copy(
        src_ref=x_hbm.at[pl.ds(frames - edge, edge)],
        dst_ref=halo,
        send_sem=halo_send,
        recv_sem=halo_recv,
        device_id={"af": af, "ta": after},
        device_id_type=MESH,
    )
    ahead.start()
    send_spectra(1, 0)
    arrange(1, 1)

    loads[3].wait()
    channelize(BLOCK, per_chunk - 1)
    ahead.wait()
    samples[pl.ds(0, edge)] = jnp.where(ta > 0, halo[...], jnp.zeros_like(halo))
    channelize(0, 1)
    arrange(0, 0)
    send_spectra(0, 0)
    send_spectra(1, 1)
    arrange(0, 1)
    send_spectra(0, 1)

    nt = (((1,), (1,)), ((), ()))

    def dot(a, b):
        return lax.dot_general(a, b, nt, preferred_element_type=jnp.float32)

    side = all_inputs // 2
    row_idx = lax.broadcasted_iota(jnp.int32, (side, side), 0)
    col_idx = lax.broadcasted_iota(jnp.int32, (side, side), 1)
    upper = row_idx <= col_idx
    lo, hi = pl.ds(0, side), pl.ds(side, side)

    def send_rows(stage, first, last):
        @pl.loop(first, last)
        def _(to_y):
            block = pl.ds(pl.multiple_of(to_y * rows, rows), rows)

            @pl.when(to_y != y)
            def _():
                pltpu.make_async_remote_copy(
                    src_ref=part.at[stage, block],
                    dst_ref=gathered.at[stage, y],
                    send_sem=row_send.at[stage],
                    recv_sem=row_recv.at[stage],
                    device_id={"af": af, "ta": to_y * 2 + z_lo},
                    device_id_type=MESH,
                ).start()

            @pl.when(to_y == y)
            def _():
                pltpu.make_async_copy(
                    part.at[stage, block], gathered.at[stage, y], row_recv.at[stage]
                ).start()

    for stage in range(STAGES):
        pltpu.make_async_copy(held.at[stage], held.at[stage], turn_recv.at[stage]).wait()
        for own, other in ((lo, hi), (hi, lo)):
            a, b = held[stage, 0, own], held[stage, 1, own]
            c, d = held[stage, 0, other], held[stage, 1, other]
            real = dot(a, a) + dot(b, b)
            imag = dot(b, a) - dot(a, b)
            part[stage, own, own] = jnp.where(upper, real, imag).astype(part.dtype)
            if own is lo:
                part[stage, own, other] = (dot(a, c) + dot(b, d)).astype(part.dtype)
                send_rows(stage, 0, NY // 2)
            else:
                part[stage, own, other] = (dot(b, c) - dot(a, d)).astype(part.dtype)
                send_rows(stage, NY // 2, NY)

    scale = 1.0 / (frames * lax.axis_size("ta"))
    own_half = pl.ds(pl.multiple_of(z_lo * half, half), half)
    other_half = pl.ds(pl.multiple_of((1 - z_lo) * half, half), half)
    for stage in range(STAGES):
        pltpu.make_async_copy(
            gathered.at[stage], gathered.at[stage], row_recv.at[stage]
        ).wait()
        acc = gathered[stage, 0].astype(jnp.float32)
        for k in range(1, NY):
            acc = acc + gathered[stage, k].astype(jnp.float32)
        total[stage] = acc * scale
        pltpu.make_async_remote_copy(
            src_ref=total.at[stage, other_half],
            dst_ref=finals.at[z_lo * STAGES + stage],
            send_sem=swap_send.at[stage],
            recv_sem=swap_recv.at[stage],
            device_id={"af": af, "ta": y * 2 + 1 - z_lo},
            device_id_type=MESH,
        ).start()
        pltpu.make_async_copy(
            total.at[stage, own_half],
            finals.at[z_lo * STAGES + stage],
            swap_recv.at[stage],
        ).start()

    for stage in range(STAGES):
        both = finals.at[pl.ds(0, 2)]
        pltpu.make_async_copy(both, both, swap_recv.at[stage]).wait()
    for k in range(2 * STAGES):
        out_ref[:, k, :] = finals[k]

    for stage in range(STAGES):
        sent = spec.at[:, stage, pl.ds(0, PEERS - 1)]
        pltpu.make_async_copy(sent, sent, turn_send.at[stage]).wait()
        sent = gathered.at[stage, pl.ds(0, NY - 1)]
        pltpu.make_async_copy(sent, sent, row_send.at[stage]).wait()
        sent = finals.at[0]
        pltpu.make_async_copy(sent, sent, swap_send.at[stage]).wait()


def on_device(samples):
    frames, inputs, samp_len = samples.shape
    all_inputs = inputs * lax.axis_size("af")
    rows = all_inputs // NY
    chunk = frames // CHUNKS
    window = jnp.asarray(tap_window(TAPS, samp_len))
    table = jnp.asarray(dft_table(samp_len, CH))
    f32, bf16 = jnp.float32, jnp.bfloat16
    dma = pltpu.SemaphoreType.DMA
    anywhere = pl.BlockSpec(memory_space=pltpu.HBM)
    return pl.pallas_call(
        correlate_kernel,
        out_shape=jax.ShapeDtypeStruct((rows // 2, 2 * STAGES, all_inputs), f32),
        in_specs=[anywhere] * 3,
        out_specs=pl.BlockSpec(memory_space=pltpu.VMEM),
        scratch_shapes=[
            pltpu.VMEM(window.shape, f32),
            pltpu.VMEM(table.shape, bf16),
            pltpu.VMEM((frames + TAPS - 1, inputs, samp_len), bf16),
            pltpu.VMEM((TAPS - 1, inputs, samp_len), bf16),
            pltpu.VMEM((BLOCK * inputs, samp_len), bf16),
            pltpu.VMEM((STAGES, chunk * inputs, 128), f32),
            pltpu.VMEM((128 * inputs, chunk), f32),
            pltpu.VMEM((CHUNKS, STAGES, PEERS, 2, inputs, chunk), bf16),
            pltpu.VMEM((STAGES, 2, all_inputs, 2 * frames), bf16),
            pltpu.VMEM((STAGES, all_inputs, all_inputs), bf16),
            pltpu.VMEM((STAGES, NY, rows, all_inputs), bf16),
            pltpu.VMEM((STAGES, rows, all_inputs), f32),
            pltpu.VMEM((2 * STAGES, rows // 2, all_inputs), f32),
            dma((4,)), dma, dma,
            dma((STAGES,)), dma((STAGES,)), dma((STAGES,)),
            dma((STAGES,)), dma((STAGES,)), dma((STAGES,)),
        ],
        compiler_params=pltpu.CompilerParams(
            collective_id=0, has_side_effects=True, vmem_limit_bytes=67_000_000
        ),
    )(samples, window, table)


def solution(mesh):
    in_specs = (P("ta", "af", None),)
    out_specs = P("ta", "af", None)
    return jax.shard_map(
        on_device, mesh=mesh, in_specs=in_specs, out_specs=out_specs, check_vma=False
    )
```

```python
import functools
import math

import jax
import jax.numpy as jnp
import numpy as np
from jax import lax
from jax.experimental import pallas as pl
from jax.experimental.pallas import tpu as pltpu
from jax.sharding import PartitionSpec as P

CH = 128
TAPS = 4
MESH = pl.DeviceIdType.MESH
NX, NZ, NY, NCORE = 4, 8, 8, 2
CHIPS = NX * NZ
PEERS = CHIPS * NCORE
STAGES = 2
CHUNKS = 2
BLOCK = 16


def tap_window(taps, samp_len):
    points = np.arange(taps * samp_len).astype(np.float64)
    centre = (taps * samp_len - 1) / 2.0
    shape_part = np.sinc((points - centre) / samp_len)
    taper = np.square(np.sin(math.pi * (points + 0.5) / (taps * samp_len)))
    return (shape_part * taper).reshape(taps, samp_len).astype(np.float32)


def dft_table(samp_len, channels):
    sample_idx = np.arange(samp_len)[:, None]
    chan_idx = np.arange(channels)[None, :]
    phase = (sample_idx * chan_idx % samp_len) * (2.0 * math.pi / samp_len)
    scale = 1.0 / math.sqrt(samp_len)
    both = np.stack([np.cos(phase) * scale, -np.sin(phase) * scale], axis=2)
    both = both.reshape(samp_len, channels // STAGES, STAGES, 2)
    both = both.transpose(0, 2, 1, 3)
    return both.reshape(samp_len, 2 * channels).astype(jnp.bfloat16)


def place():
    af, ta = lax.axis_index("af"), lax.axis_index("ta")
    z = lax.div(af, 8) * 2 + lax.rem(ta, 2)
    return z, lax.rem(lax.div(af, 2), NX), lax.rem(af, 2), lax.div(ta, 2)


def turn_peer(turn, along_x, core):
    z, x, _, y = place()
    odd = lax.rem(turn, 2)
    hop = lax.div(turn + 1, 2)
    z = lax.rem(z + odd * hop + (1 - odd) * (NZ - hop), NZ)
    x = lax.rem(x + along_x, NX)
    z_lo = lax.rem(z, 2)
    return lax.div(z, 2) * 8 + x * 2 + core, y * 2 + z_lo, z_lo


def correlate_kernel(
    x_hbm, w_hbm, t_hbm, out_ref,
    window, table, samples, halo, filtered, spectra, turned, spec,
    held, part, gathered, total, finals,
    load_sem, halo_send, halo_recv,
    turn_send, turn_recv, row_send, row_recv, swap_send, swap_recv,
):
    z, x, core, y = place()
    af, ta = lax.axis_index("af"), lax.axis_index("ta")
    z_lo = lax.rem(z, 2)
    n_ta = lax.axis_size("ta")
    frames, inputs, samp_len = x_hbm.shape
    edge = TAPS - 1
    chunk = frames // CHUNKS
    all_inputs = held.shape[2]
    rows = all_inputs // NY
    half = rows // 2

    window_load = pltpu.make_async_copy(w_hbm, window, load_sem.at[0])
    table_load = pltpu.make_async_copy(t_hbm, table, load_sem.at[1])

    def load(first, count, sem):
        return pltpu.make_async_copy(
            x_hbm.at[pl.ds(first, count)],
            samples.at[pl.ds(first + edge, count)],
            load_sem.at[sem],
        )

    window_load.start()
    load(chunk - edge, edge, 2).start()
    per_chunk = chunk // BLOCK
    load(chunk, BLOCK, 4).start()
    table_load.start()
    for step in range(1, per_chunk):
        load(chunk + step * BLOCK, BLOCK, 4 + step).start()
    load(0, chunk - edge, 3).start()

    barrier = pltpu.get_barrier_semaphore()

    def greet(to_af, to_ta):
        pl.semaphore_signal(
            barrier, inc=1, device_id={"af": to_af, "ta": to_ta}, device_id_type=MESH
        )

    @pl.loop(0, (NZ - 1) * NX)
    def _(step):
        for to_core in range(NCORE):
            along_x = lax.rem(6 - lax.rem(step, NX), NX)
            to_af, to_ta, _ = turn_peer(NZ - 1 - lax.div(step, NX), along_x, to_core)
            greet(to_af, to_ta)

    for along_x in (2, 1, 3):
        for to_core in range(NCORE):
            to_af, to_ta, _ = turn_peer(0, along_x, to_core)
            greet(to_af, to_ta)
    greet(af + 1 - 2 * core, ta)

    @pl.loop(1, NY)
    def _(step):
        greet(af, lax.rem(y + step, NY) * 2 + z_lo)

    after, before = lax.rem(ta + 1, n_ta), lax.rem(ta + n_ta - 1, n_ta)
    greet(af, after)
    greet(af, before)
    n_greet = PEERS - 1 + NY - 1 + 2

    my_rows = pl.ds(pl.multiple_of(af * inputs, inputs), inputs)

    def send_spectra(stage, to_core, first, count):
        lanes = pl.ds(first, count)
        start = pl.multiple_of(z_lo * frames + first, chunk)
        target = held.at[stage, :, my_rows, pl.ds(start, count)]

        def send(step):
            to_af, to_ta, to_lo = turn_peer(lax.rem(step, NZ), lax.div(step, NZ), to_core)
            pltpu.make_async_remote_copy(
                src_ref=spec.at[stage, to_af * 2 + to_lo, :, :, lanes],
                dst_ref=target,
                send_sem=turn_send.at[stage],
                recv_sem=turn_recv.at[stage],
                device_id={"af": to_af, "ta": to_ta},
                device_id_type=MESH,
            ).start()

        pl.loop(1, CHIPS)(send)

        @pl.when(core != to_core)
        def _():
            send(0)

        @pl.when(core == to_core)
        def _():
            pltpu.make_async_copy(
                spec.at[stage, af * 2 + z_lo, :, :, lanes], target, turn_recv.at[stage]
            ).start()

    def channelize(first, count, arriving=False):
        base = first // chunk * chunk

        @pl.loop(0, count)
        def _(step):
            if arriving:
                f0 = first + step * BLOCK
                load(0, BLOCK, 4 + step).wait()
            else:
                f0 = first + (count - 1 - step) * BLOCK
            for lane in range(samp_len // 128):
                cols = pl.ds(lane * 128, 128)
                taps = [
                    jnp.broadcast_to(window[pl.ds(p, 1), cols], (inputs, 128))
                    for p in range(TAPS)
                ]
                recent = [samples[f0 + p, :, cols].astype(jnp.float32) for p in range(edge)]
                for f in range(BLOCK):
                    recent.append(samples[f0 + f + edge, :, cols].astype(jnp.float32))
                    acc = taps[0] * recent[0]
                    for p in range(1, TAPS):
                        acc = acc + taps[p] * recent[p]
                    filtered[pl.ds(f * inputs, inputs), cols] = acc.astype(jnp.bfloat16)
                    recent = recent[1:]
            block = jnp.dot(filtered[...], table[...], preferred_element_type=jnp.float32)
            at = pl.ds(pl.multiple_of((f0 - base) * inputs, BLOCK * inputs), BLOCK * inputs)
            for stage in range(STAGES):
                spectra[stage, at, :] = block[:, stage * 128 : (stage + 1) * 128]

    def arrange(k, stage):
        for i in range(inputs):
            by_frame = spectra[stage, pl.ds(i, chunk, stride=inputs), :]
            turned[pl.ds(i, 128, stride=inputs), :] = by_frame.T
        pieces = turned[...].astype(jnp.bfloat16)
        spec[stage, :, :, :, pl.ds(k * chunk, chunk)] = pieces.reshape(PEERS, 2, inputs, chunk)

    window_load.wait()
    load(chunk - edge, edge, 2).wait()
    table_load.wait()
    channelize(chunk, per_chunk, arriving=True)
    arrange(1, 0)

    pl.semaphore_wait(barrier, n_greet)
    ahead = pltpu.make_async_remote_copy(
        src_ref=x_hbm.at[pl.ds(frames - edge, edge)],
        dst_ref=halo,
        send_sem=halo_send,
        recv_sem=halo_recv,
        device_id={"af": af, "ta": after},
        device_id_type=MESH,
    )
    ahead.start()
    send_spectra(0, 0, chunk, chunk)
    send_spectra(0, 1, chunk, chunk)
    arrange(1, 1)

    load(0, chunk - edge, 3).wait()
    channelize(BLOCK, per_chunk - 1)
    ahead.wait()
    samples[pl.ds(0, edge)] = jnp.where(ta > 0, halo[...], jnp.zeros_like(halo))
    channelize(0, 1)
    arrange(0, 0)
    send_spectra(0, 0, 0, chunk)
    send_spectra(0, 1, 0, chunk)
    arrange(0, 1)
    send_spectra(1, 0, 0, frames)
    send_spectra(1, 1, 0, frames)

    nt = (((1,), (1,)), ((), ()))

    def dot(a, b):
        return lax.dot_general(a, b, nt, preferred_element_type=jnp.float32)

    side = all_inputs // 2
    row_idx = lax.broadcasted_iota(jnp.int32, (side, side), 0)
    col_idx = lax.broadcasted_iota(jnp.int32, (side, side), 1)
    upper = row_idx <= col_idx
    lo, hi = pl.ds(0, side), pl.ds(side, side)

    def send_rows(stage):
        @pl.loop(0, NY - 1)
        def _(step):
            odd = lax.rem(step, 2)
            hop = NY // 2 - lax.div(step + 1, 2)
            to_y = lax.rem(y + odd * hop + (1 - odd) * (NY - hop), NY)
            block = pl.ds(pl.multiple_of(to_y * rows, rows), rows)
            pltpu.make_async_remote_copy(
                src_ref=part.at[stage, block],
                dst_ref=gathered.at[stage, y],
                send_sem=row_send.at[stage],
                recv_sem=row_recv.at[stage],
                device_id={"af": af, "ta": to_y * 2 + z_lo},
                device_id_type=MESH,
            ).start()

        own = pl.ds(pl.multiple_of(y * rows, rows), rows)
        pltpu.make_async_copy(
            part.at[stage, own], gathered.at[stage, y], row_recv.at[stage]
        ).start()

    for stage in range(STAGES):
        pltpu.make_async_copy(held.at[stage], held.at[stage], turn_recv.at[stage]).wait()
        for own, other in ((lo, hi), (hi, lo)):
            a, b = held[stage, 0, own], held[stage, 1, own]
            c, d = held[stage, 0, other], held[stage, 1, other]
            real = dot(a, a) + dot(b, b)
            imag = dot(b, a) - dot(a, b)
            part[stage, own, own] = jnp.where(upper, real, imag).astype(part.dtype)
            if own is lo:
                part[stage, own, other] = (dot(a, c) + dot(b, d)).astype(part.dtype)
            else:
                part[stage, own, other] = (dot(b, c) - dot(a, d)).astype(part.dtype)
                send_rows(stage)

    scale = 1.0 / (frames * lax.axis_size("ta"))
    own_half = pl.ds(pl.multiple_of(z_lo * half, half), half)
    other_half = pl.ds(pl.multiple_of((1 - z_lo) * half, half), half)
    for stage in range(STAGES):
        pltpu.make_async_copy(
            gathered.at[stage], gathered.at[stage], row_recv.at[stage]
        ).wait()
        acc = gathered[stage, 0].astype(jnp.float32)
        for k in range(1, NY):
            acc = acc + gathered[stage, k].astype(jnp.float32)
        total[stage] = acc * scale
        pltpu.make_async_remote_copy(
            src_ref=total.at[stage, other_half],
            dst_ref=finals.at[z_lo * STAGES + stage],
            send_sem=swap_send.at[stage],
            recv_sem=swap_recv.at[stage],
            device_id={"af": af, "ta": y * 2 + 1 - z_lo},
            device_id_type=MESH,
        ).start()
        pltpu.make_async_copy(
            total.at[stage, own_half],
            finals.at[z_lo * STAGES + stage],
            swap_recv.at[stage],
        ).start()

    for stage in range(STAGES):
        both = finals.at[pl.ds(0, 2)]
        pltpu.make_async_copy(both, both, swap_recv.at[stage]).wait()
    for k in range(2 * STAGES):
        out_ref[:, k, :] = finals[k]

    for stage in range(STAGES):
        sent = spec.at[stage, pl.ds(0, PEERS - 1)]
        pltpu.make_async_copy(sent, sent, turn_send.at[stage]).wait()
        sent = gathered.at[stage, pl.ds(0, NY - 1)]
        pltpu.make_async_copy(sent, sent, row_send.at[stage]).wait()
        sent = finals.at[0]
        pltpu.make_async_copy(sent, sent, swap_send.at[stage]).wait()


def on_device(samples):
    frames, inputs, samp_len = samples.shape
    all_inputs = inputs * lax.axis_size("af")
    rows = all_inputs // NY
    chunk = frames // CHUNKS
    window = jnp.asarray(tap_window(TAPS, samp_len))
    table = jnp.asarray(dft_table(samp_len, CH))
    f32, bf16 = jnp.float32, jnp.bfloat16
    dma = pltpu.SemaphoreType.DMA
    anywhere = pl.BlockSpec(memory_space=pltpu.HBM)
    return pl.pallas_call(
        correlate_kernel,
        out_shape=jax.ShapeDtypeStruct((rows // 2, 2 * STAGES, all_inputs), f32),
        in_specs=[anywhere] * 3,
        out_specs=pl.BlockSpec(memory_space=pltpu.VMEM),
        scratch_shapes=[
            pltpu.VMEM(window.shape, f32),
            pltpu.VMEM(table.shape, bf16),
            pltpu.VMEM((frames + TAPS - 1, inputs, samp_len), bf16),
            pltpu.VMEM((TAPS - 1, inputs, samp_len), bf16),
            pltpu.VMEM((BLOCK * inputs, samp_len), bf16),
            pltpu.VMEM((STAGES, chunk * inputs, 128), f32),
            pltpu.VMEM((128 * inputs, chunk), f32),
            pltpu.VMEM((STAGES, PEERS, 2, inputs, frames), bf16),
            pltpu.VMEM((STAGES, 2, all_inputs, 2 * frames), bf16),
            pltpu.VMEM((STAGES, all_inputs, all_inputs), bf16),
            pltpu.VMEM((STAGES, NY, rows, all_inputs), bf16),
            pltpu.VMEM((STAGES, rows, all_inputs), f32),
            pltpu.VMEM((2 * STAGES, rows // 2, all_inputs), f32),
            dma((4 + chunk // BLOCK,)), dma, dma,
            dma((STAGES,)), dma((STAGES,)), dma((STAGES,)),
            dma((STAGES,)), dma((STAGES,)), dma((STAGES,)),
        ],
        compiler_params=pltpu.CompilerParams(
            collective_id=0, has_side_effects=True, vmem_limit_bytes=67_000_000
        ),
    )(samples, window, table)


def solution(mesh):
    in_specs = (P("ta", "af", None),)
    out_specs = P("ta", "af", None)
    return jax.shard_map(
        on_device, mesh=mesh, in_specs=in_specs, out_specs=out_specs, check_vma=False
    )
```

```python
import functools
import math

import jax
import jax.numpy as jnp
import numpy as np
from jax import lax
from jax.experimental import pallas as pl
from jax.experimental.pallas import tpu as pltpu
from jax.sharding import PartitionSpec as P

CH = 128
TAPS = 4
MESH = pl.DeviceIdType.MESH
NX, NZ, NY, NCORE = 4, 8, 8, 2
N_ZHI = NZ // 2
NEAR, FAR = (0, 1, 3), 2
CHIPS = NX * NZ
PEERS = CHIPS * NCORE
STAGES = 2
CHUNKS = 2
BLOCK = 16


def tap_window(taps, samp_len):
    points = np.arange(taps * samp_len).astype(np.float64)
    centre = (taps * samp_len - 1) / 2.0
    shape_part = np.sinc((points - centre) / samp_len)
    taper = np.square(np.sin(math.pi * (points + 0.5) / (taps * samp_len)))
    return (shape_part * taper).reshape(taps, samp_len).astype(np.float32)


def dft_table(samp_len, channels):
    sample_idx = np.arange(samp_len)[:, None]
    chan_idx = np.arange(channels)[None, :]
    phase = (sample_idx * chan_idx % samp_len) * (2.0 * math.pi / samp_len)
    scale = 1.0 / math.sqrt(samp_len)
    both = np.stack([np.cos(phase) * scale, -np.sin(phase) * scale], axis=2)
    both = both.reshape(samp_len, channels // STAGES, STAGES, 2)
    both = both.transpose(0, 2, 1, 3)
    return both.reshape(samp_len, 2 * channels).astype(jnp.bfloat16)


def place():
    af, ta = lax.axis_index("af"), lax.axis_index("ta")
    z = lax.div(af, 8) * 2 + lax.rem(ta, 2)
    return z, lax.rem(lax.div(af, 2), NX), lax.rem(af, 2), lax.div(ta, 2)


def turn_peer(turn, along_x, core):
    z, x, _, y = place()
    odd = lax.rem(turn, 2)
    hop = lax.div(turn + 1, 2)
    z = lax.rem(z + odd * hop + (1 - odd) * (NZ - hop), NZ)
    x = lax.rem(x + along_x, NX)
    z_lo = lax.rem(z, 2)
    return lax.div(z, 2) * 8 + x * 2 + core, y * 2 + z_lo, z_lo


def correlate_kernel(
    x_hbm, w_hbm, t_hbm, out_ref,
    window, table, samples, halo, filtered, spectra, turned, spec,
    held, part, gathered, total, finals,
    load_sem, halo_send, halo_recv,
    turn_send, turn_recv, row_send, row_recv, swap_send, swap_recv,
):
    z, x, core, y = place()
    af, ta = lax.axis_index("af"), lax.axis_index("ta")
    z_lo = lax.rem(z, 2)
    n_ta = lax.axis_size("ta")
    frames, inputs, samp_len = x_hbm.shape
    edge = TAPS - 1
    chunk = frames // CHUNKS
    all_inputs = held.shape[2]
    rows = all_inputs // NY
    half = rows // 2

    window_load = pltpu.make_async_copy(w_hbm, window, load_sem.at[0])
    table_load = pltpu.make_async_copy(t_hbm, table, load_sem.at[1])

    def load(first, count, sem):
        return pltpu.make_async_copy(
            x_hbm.at[pl.ds(first, count)],
            samples.at[pl.ds(first + edge, count)],
            load_sem.at[sem],
        )

    window_load.start()
    load(chunk - edge, edge, 2).start()
    per_chunk = chunk // BLOCK
    load(chunk, BLOCK, 4).start()
    table_load.start()
    for step in range(1, per_chunk):
        load(chunk + step * BLOCK, BLOCK, 4 + step).start()
    load(0, chunk - edge, 3).start()

    barrier = pltpu.get_barrier_semaphore()

    def greet(to_af, to_ta):
        pl.semaphore_signal(
            barrier, inc=1, device_id={"af": to_af, "ta": to_ta}, device_id_type=MESH
        )

    @pl.loop(0, (NZ - 1) * NX)
    def _(step):
        for to_core in range(NCORE):
            along_x = lax.rem(6 - lax.rem(step, NX), NX)
            to_af, to_ta, _ = turn_peer(NZ - 1 - lax.div(step, NX), along_x, to_core)
            greet(to_af, to_ta)

    for along_x in (2, 1, 3):
        for to_core in range(NCORE):
            to_af, to_ta, _ = turn_peer(0, along_x, to_core)
            greet(to_af, to_ta)
    greet(af + 1 - 2 * core, ta)

    @pl.loop(1, NY)
    def _(step):
        greet(af, lax.rem(y + step, NY) * 2 + z_lo)

    after, before = lax.rem(ta + 1, n_ta), lax.rem(ta + n_ta - 1, n_ta)
    greet(af, after)
    greet(af, before)
    n_greet = PEERS - 1 + NY - 1 + 2

    my_slot = (x * N_ZHI + lax.div(z, 2)) * NCORE + core
    my_rows = pl.ds(pl.multiple_of(my_slot * inputs, inputs), inputs)

    def send_spectra(stage, to_core, first, count):
        lanes = pl.ds(first, count)
        start = pl.multiple_of(z_lo * frames + first, chunk)
        target = held.at[stage, :, my_rows, pl.ds(start, count)]
        far_sem = turn_recv.at[STAGES if stage == STAGES - 1 else stage]

        def send(step, along_x, recv_sem):
            to_af, to_ta, to_lo = turn_peer(step, along_x, to_core)
            pltpu.make_async_remote_copy(
                src_ref=spec.at[stage, to_af * 2 + to_lo, :, :, lanes],
                dst_ref=target,
                send_sem=turn_send.at[stage],
                recv_sem=recv_sem,
                device_id={"af": to_af, "ta": to_ta},
                device_id_type=MESH,
            ).start()

        @pl.loop(1, len(NEAR) * NZ)
        def _(step):
            group = lax.div(step, NZ)
            send(lax.rem(step, NZ), group + lax.div(group, 2), turn_recv.at[stage])

        @pl.when(core != to_core)
        def _():
            send(0, 0, turn_recv.at[stage])

        @pl.when(core == to_core)
        def _():
            pltpu.make_async_copy(
                spec.at[stage, af * 2 + z_lo, :, :, lanes], target, turn_recv.at[stage]
            ).start()

        @pl.loop(0, NZ)
        def _(step):
            send(step, FAR, far_sem)

    def channelize(first, count, arriving=False):
        base = first // chunk * chunk

        @pl.loop(0, count)
        def _(step):
            if arriving:
                f0 = first + step * BLOCK
                load(0, BLOCK, 4 + step).wait()
            else:
                f0 = first + (count - 1 - step) * BLOCK
            for lane in range(samp_len // 128):
                cols = pl.ds(lane * 128, 128)
                taps = [
                    jnp.broadcast_to(window[pl.ds(p, 1), cols], (inputs, 128))
                    for p in range(TAPS)
                ]
                recent = [samples[f0 + p, :, cols].astype(jnp.float32) for p in range(edge)]
                for f in range(BLOCK):
                    recent.append(samples[f0 + f + edge, :, cols].astype(jnp.float32))
                    acc = taps[0] * recent[0]
                    for p in range(1, TAPS):
                        acc = acc + taps[p] * recent[p]
                    filtered[pl.ds(f * inputs, inputs), cols] = acc.astype(jnp.bfloat16)
                    recent = recent[1:]
            block = jnp.dot(filtered[...], table[...], preferred_element_type=jnp.float32)
            at = pl.ds(pl.multiple_of((f0 - base) * inputs, BLOCK * inputs), BLOCK * inputs)
            for stage in range(STAGES):
                spectra[stage, at, :] = block[:, stage * 128 : (stage + 1) * 128]

    def arrange(k, stage):
        for i in range(inputs):
            by_frame = spectra[stage, pl.ds(i, chunk, stride=inputs), :]
            turned[pl.ds(i, 128, stride=inputs), :] = by_frame.T
        pieces = turned[...].astype(jnp.bfloat16)
        spec[stage, :, :, :, pl.ds(k * chunk, chunk)] = pieces.reshape(PEERS, 2, inputs, chunk)

    window_load.wait()
    load(chunk - edge, edge, 2).wait()
    table_load.wait()
    channelize(chunk, per_chunk, arriving=True)
    arrange(1, 0)

    pl.semaphore_wait(barrier, n_greet)
    ahead = pltpu.make_async_remote_copy(
        src_ref=x_hbm.at[pl.ds(frames - edge, edge)],
        dst_ref=halo,
        send_sem=halo_send,
        recv_sem=halo_recv,
        device_id={"af": af, "ta": after},
        device_id_type=MESH,
    )
    ahead.start()
    send_spectra(0, 0, chunk, chunk)
    send_spectra(0, 1, chunk, chunk)
    arrange(1, 1)

    load(0, chunk - edge, 3).wait()
    channelize(BLOCK, per_chunk - 1)
    ahead.wait()
    samples[pl.ds(0, edge)] = jnp.where(ta > 0, halo[...], jnp.zeros_like(halo))
    channelize(0, 1)
    arrange(0, 0)
    send_spectra(0, 0, 0, chunk)
    send_spectra(0, 1, 0, chunk)
    arrange(0, 1)
    send_spectra(1, 0, 0, frames)
    send_spectra(1, 1, 0, frames)

    nt = (((1,), (1,)), ((), ()))

    def dot(a, b):
        return lax.dot_general(a, b, nt, preferred_element_type=jnp.float32)

    group = all_inputs // NX
    gap = lax.broadcasted_iota(jnp.int32, (half, group), 0)
    lane = lax.broadcasted_iota(jnp.int32, (half, group), 1)
    gap = gap - (lane // half * group + lane % half)

    def products(stage, row_groups, col_groups):
        def rows_of(groups, half_of):
            starts = [pl.multiple_of(g * group, group) for g in groups]
            return jnp.concatenate([held[stage, half_of, pl.ds(g, group)] for g in starts], axis=0)

        a, b = (rows_of(row_groups, k) for k in range(2))
        c, d = (rows_of(col_groups, k) for k in range(2))
        return dot(a, c) + dot(b, d), dot(b, c) - dot(a, d)

    def pack(stage, row_groups, col_groups, at, real, imag):
        for m, row_group in enumerate(row_groups):
            for block in range(N_ZHI):
                r0 = m * group + block * half
                for n, col_group in enumerate(col_groups):
                    upper = gap <= half * (col_group - row_group) - block * group
                    here = (slice(r0, r0 + half), slice(n * group, (n + 1) * group))
                    lanes = pl.ds((at + n) * group, group)
                    part[stage, row_group, block, :, lanes] = jnp.where(
                        upper, real[here], imag[here]
                    ).astype(part.dtype)

    def send_rows(stage, to_y, source, target):
        @pl.when(to_y != y)
        def _():
            pltpu.make_async_remote_copy(
                src_ref=source,
                dst_ref=target,
                send_sem=row_send.at[stage],
                recv_sem=row_recv.at[stage],
                device_id={"af": af, "ta": to_y * 2 + z_lo},
                device_id_type=MESH,
            ).start()

        @pl.when(to_y == y)
        def _():
            pltpu.make_async_copy(source, target, row_recv.at[stage]).start()

    def send_groups(stage, pieces):
        @pl.loop(0, N_ZHI)
        def _(step):
            late = lax.div(step, 2)
            ahead = (1 - late) * (2 + step) + late * (3 - step)
            block = lax.rem(lax.div(y, 2) + ahead, N_ZHI)
            for row_group, lanes in pieces:
                send_rows(
                    stage,
                    block * 2 + lax.div(row_group, 2),
                    part.at[stage, row_group, block, :, lanes],
                    gathered.at[stage, y, lax.rem(row_group, 2), :, lanes],
                )

    scale = 1.0 / (frames * n_ta)

    def add_up(stage, place_of):
        pltpu.make_async_copy(
            gathered.at[stage], gathered.at[stage], row_recv.at[stage]
        ).wait()
        lane_group = lane // half

        def half_sum(part_of):
            sums = []
            for g in range(NX):
                lanes = pl.ds(pl.multiple_of(place_of(g) * group, group), group)
                acc = gathered[stage, 0, part_of, :, lanes].astype(jnp.float32)
                for k in range(1, NY):
                    acc = acc + gathered[stage, k, part_of, :, lanes].astype(jnp.float32)
                sums.append(acc * scale)
            for block in range(N_ZHI):
                tile = sums[0] if block == 0 else pltpu.roll(sums[0], group - block * half, 1)
                for g in range(1, NX):
                    shift = (g - block) * half % group
                    moved = pltpu.roll(sums[g], shift, 1) if shift else sums[g]
                    tile = jnp.where(lane_group == g, moved, tile)
                yield pl.ds(block * group, group), tile

        for lanes, tile in half_sum(1 - z_lo):
            total[stage, :, lanes] = tile
        slot = z_lo * STAGES + stage
        pltpu.make_async_remote_copy(
            src_ref=total.at[stage],
            dst_ref=finals.at[slot],
            send_sem=swap_send.at[stage],
            recv_sem=swap_recv.at[stage],
            device_id={"af": af, "ta": y * 2 + 1 - z_lo},
            device_id_type=MESH,
        ).start()
        for lanes, tile in half_sum(z_lo):
            finals[slot, :, lanes] = tile

    def finish(stage):
        pltpu.make_async_copy(finals.at[0], finals.at[0], swap_recv.at[stage]).wait()
        for k in (stage, STAGES + stage):
            out_ref[:, k, :] = finals[k]

    pltpu.make_async_copy(held.at[0], held.at[0], turn_recv.at[0]).wait()
    every = tuple(range(NX))
    for row_groups in (every[: NX // 2], every[NX // 2 :]):
        pack(0, row_groups, every, 0, *products(0, row_groups, every))

    @pl.loop(0, NY)
    def _(step):
        odd = lax.rem(step, 2)
        hop = NY // 2 - lax.div(step + 1, 2)
        to_y = lax.rem(y + odd * hop + (1 - odd) * (NY - hop), NY)
        source = part.at[0, pl.ds(lax.rem(to_y, 2) * 2, 2), lax.div(to_y, 2)]
        send_rows(0, to_y, source, gathered.at[0, y])

    near = [lax.rem(x + d, NX) for d in NEAR]
    far = lax.rem(x + FAR, NX)
    n_near = len(NEAR)
    last = STAGES - 1
    arrived = held.at[last, :, pl.ds(0, n_near * group)]
    pltpu.make_async_copy(arrived, arrived, turn_recv.at[last]).wait()
    pack(last, near, near, 0, *products(last, near, near))
    send_groups(last, [(g, pl.ds(0, n_near * group)) for g in near])

    arrived = held.at[last, :, pl.ds(0, group)]
    pltpu.make_async_copy(arrived, arrived, turn_recv.at[STAGES]).wait()
    real, imag = products(last, near + [far], [far])
    pack(last, [far], near, 0, real[: n_near * group].T, -imag[: n_near * group].T)
    pack(last, near + [far], [far], n_near, real, imag)
    pieces = [(g, pl.ds(n_near * group, group)) for g in near]
    send_groups(last, [(far, pl.ds(0, all_inputs))] + pieces)

    add_up(0, lambda g: g)
    finish(0)

    def place_of(g):
        d = lax.rem(g - x + NX, NX)
        return d + lax.div(d, 2) * (5 - 2 * d)

    add_up(last, place_of)

    finish(last)

    for stage in range(STAGES):
        sent = spec.at[stage, pl.ds(0, PEERS - 1)]
        pltpu.make_async_copy(sent, sent, turn_send.at[stage]).wait()
        sent = gathered.at[stage, pl.ds(0, NY - 1)]
        pltpu.make_async_copy(sent, sent, row_send.at[stage]).wait()
        sent = total.at[stage]
        pltpu.make_async_copy(sent, sent, swap_send.at[stage]).wait()


def on_device(samples):
    frames, inputs, samp_len = samples.shape
    all_inputs = inputs * lax.axis_size("af")
    rows = all_inputs // NY
    chunk = frames // CHUNKS
    window = jnp.asarray(tap_window(TAPS, samp_len))
    table = jnp.asarray(dft_table(samp_len, CH))
    f32, bf16 = jnp.float32, jnp.bfloat16
    dma = pltpu.SemaphoreType.DMA
    anywhere = pl.BlockSpec(memory_space=pltpu.HBM)
    return pl.pallas_call(
        correlate_kernel,
        out_shape=jax.ShapeDtypeStruct((rows // 2, 2 * STAGES, all_inputs), f32),
        in_specs=[anywhere] * 3,
        out_specs=pl.BlockSpec(memory_space=pltpu.VMEM),
        scratch_shapes=[
            pltpu.VMEM(window.shape, f32),
            pltpu.VMEM(table.shape, bf16),
            pltpu.VMEM((frames + TAPS - 1, inputs, samp_len), bf16),
            pltpu.VMEM((TAPS - 1, inputs, samp_len), bf16),
            pltpu.VMEM((BLOCK * inputs, samp_len), bf16),
            pltpu.VMEM((STAGES, chunk * inputs, 128), f32),
            pltpu.VMEM((128 * inputs, chunk), f32),
            pltpu.VMEM((STAGES, PEERS, 2, inputs, frames), bf16),
            pltpu.VMEM((STAGES, 2, all_inputs, 2 * frames), bf16),
            pltpu.VMEM((STAGES, NX, N_ZHI, rows // 2, all_inputs), bf16),
            pltpu.VMEM((STAGES, NY, 2, rows // 2, all_inputs), bf16),
            pltpu.VMEM((STAGES, rows // 2, all_inputs), f32),
            pltpu.VMEM((2 * STAGES, rows // 2, all_inputs), f32),
            dma((4 + chunk // BLOCK,)), dma, dma,
            dma((STAGES,)), dma((STAGES + 1,)), dma((STAGES,)),
            dma((STAGES,)), dma((STAGES,)), dma((STAGES,)),
        ],
        compiler_params=pltpu.CompilerParams(
            collective_id=0, has_side_effects=True, vmem_limit_bytes=67_000_000
        ),
    )(samples, window, table)


def solution(mesh):
    in_specs = (P("ta", "af", None),)
    out_specs = P("ta", "af", None)
    return jax.shard_map(
        on_device, mesh=mesh, in_specs=in_specs, out_specs=out_specs, check_vma=False
    )
```
